32 devices in a mesh: parts: 2 (over y), blk: 4 (over z), win: 2 (over x), bin: 2 (over core).
Axes of the slice: x: 2, y: 2, z: 4, core: 2. Of those that a mesh axis runs over, the one named last changes fastest.
Arguments:
- raw_counts: bfloat16 [2400, 8, 640], P(('win', 'bin'), ('parts', 'blk')), parts along dimension 1, may hold values from -6 to 6
- seg_valid: int32 [4, 512], P(('win', 'bin'), ('parts', 'blk')), parts along dimension 1, may hold values 0 or 1
Outputs:
- pair_stacks: float32 [2, 8, 2, 320, 4096], P(None, ('parts', 'blk'), None, ('win', 'bin')), parts along dimension 1
The draws below stay inside these ranges and needn't reach their ends.
There are 2 independent parts, one for each index of `parts`. The reference program is written for one: setup_inputs(seed, part) draws one part's arguments, and reference() takes and returns one part's arrays. A program takes and returns all parts, laid end to end along the dimension named above; each array names one. Nothing has to cross between parts.
All inputs are finite; a program needn't handle non-finite values. No bound on the sum of `seg_valid` on one device may be relied on, other than what follows from the above.
Results may differ from the reference program's by a relative error of at most 0.006.
Values may be sent and summed in bfloat16 or wider, within the bound.
No kernel may reach another device: no remote copies, remote signals or barrier semaphores. Data moves between devices by JAX's collectives and lax.ppermute only.
A program may use at most 64 MiB of HBM per device.

```python
import math
import jax
import jax.numpy as jnp
from jax import lax

SB = 64
LSEG = 600
NF = 320
DECIM = 10
TAPS = 64
SMOOTH = 33
ROUNDS = 2
HIST = 7
NBLK = 4
STATIONS = 256
SEGS = 4
ROWS = 2400


def with_ends(drawn, own_key, smallest, largest):
    longest = drawn.shape.index(max(drawn.shape))
    spots = []
    for shift in (0, 1):
        where = [jax.random.randint(jax.random.fold_in(own_key, axis), (), 0, length) for axis, length in enumerate(drawn.shape)]
        where[longest] = (where[longest] + shift) % drawn.shape[longest]
        spots.append(tuple(where))
    return drawn.at[spots[0]].set(smallest).at[spots[1]].set(largest)


def steps_of(rng, extent, split, smallest, top_value):
    def one(axis_at, shards_of):
        heights = jax.random.uniform(jax.random.fold_in(jax.random.fold_in(rng, 6), axis_at), (shards_of,), jnp.float32, smallest / len(split), top_value / len(split))
        return jnp.repeat(jnp.exp(heights), extent[axis_at] // shards_of).reshape((-1,) + (1,) * (len(extent) - axis_at - 1))

    level = one(*split[0])
    for cut in split[1:]:
        level = level * one(*cut)
    return level


def bell_draw(own_key, dims, spread, bound, split=(), kind=jnp.bfloat16):
    entries = jax.random.normal(own_key, dims, jnp.float32) * spread
    if len(split) > 0:
        entries = steps_of(own_key, dims, split, -0.22, 0.18) * entries
    return jnp.clip(entries, min=-bound, max=bound).astype(kind)


def setup_inputs(seed: int = 0, part: int = 0) -> dict:
    seeds = jax.random.split(jax.random.key(seed), 3)
    part_keys = jax.random.split(jax.random.fold_in(seeds[2], part), 3)
    return {
        "raw_counts": bell_draw(part_keys[0], (ROWS, NBLK, DECIM * SB), 1.0, 6.0, ((0, 4), (1, 4))),
        "seg_valid": with_ends((jax.random.randint(part_keys[1], (SEGS, STATIONS), 0, 8) < 7).astype(jnp.int32), jax.random.fold_in(part_keys[1], 1), 0, 1),
    }


epsilon = 1e-06

def filter_coeffs():
    position = jnp.arange(TAPS, dtype=jnp.int32).astype(jnp.float32)
    centre = 0.5 * (TAPS - 1)
    cutoff = 0.4 / DECIM
    shaped = jnp.sinc(2.0 * cutoff * (position - centre))
    window = 0.54 - 0.46 * jnp.cos(2.0 * math.pi * position / (TAPS - 1))
    return 2.0 * cutoff * shaped * window

def polyphase():
    coeffs = filter_coeffs()
    delays = DECIM * jnp.arange(HIST + 1, dtype=jnp.int32)[:, None] - jnp.arange(DECIM, dtype=jnp.int32)[None, :]
    matches = delays[:, :, None] == jnp.arange(TAPS, dtype=jnp.int32)[None, None, :]
    return lax.optimization_barrier(jnp.sum(jnp.where(matches, coeffs[None, None, :], 0.0), axis=2))

def fourier_table():
    row_index = jnp.arange(2 * NF, dtype=jnp.int32)
    frequency = row_index // 2 + 1
    component = row_index % 2
    position = jnp.arange(LSEG, dtype=jnp.int32)
    phase_step = frequency[:, None] * position[None, :] % (2 * LSEG)
    radians = phase_step.astype(jnp.float32) * (math.pi / LSEG)
    return jnp.where(component[:, None] == 0, jnp.cos(radians), -jnp.sin(radians)).astype(jnp.bfloat16)

def smoother():
    row_index = jnp.arange(NF, dtype=jnp.int32)
    first_bin = jnp.clip(row_index - SMOOTH // 2, 0, NF - SMOOTH)
    columns = jnp.arange(NF, dtype=jnp.int32)[None, :]
    inside = (columns >= first_bin[:, None]) & (columns < first_bin[:, None] + SMOOTH)
    return inside.astype(jnp.float32)

def decimate(samples, history):
    row_count = samples.shape[0]
    extended = jnp.concatenate([history, samples], 0).astype(jnp.float32)
    extended = extended.reshape(row_count + HIST, DECIM, SB)
    weights = polyphase()
    running = jnp.zeros((row_count, SB), jnp.float32)
    for offset_back in range(HIST + 1):
        window_rows = extended[HIST - offset_back:HIST - offset_back + row_count]
        running = running + lax.optimization_barrier(jnp.sum(window_rows * weights[offset_back][None, :, None], axis=1))
    return running.astype(jnp.bfloat16)

def whiten(decimated, validity):
    segments = decimated.shape[0] // LSEG
    framed = decimated.reshape(segments, LSEG, SB).astype(jnp.float32)
    spectra = jnp.einsum('kn,sni->ski', fourier_table().astype(jnp.float32), framed)
    paired = spectra.reshape(segments, NF, 2, SB)
    energy = lax.optimization_barrier(jnp.sum(paired * paired, axis=2))
    smoothed = jnp.einsum('fg,sgi->sfi', smoother(), energy, precision=lax.Precision.HIGHEST) / (2.0 * SMOOTH)
    scaling = validity.astype(jnp.float32)[:, None, :] / jnp.sqrt(smoothed + epsilon)
    return (paired * scaling[:, :, None, :]).astype(jnp.bfloat16).reshape(segments, NF, 2 * SB)

def cross_block(home_spec, away_spec, seg_total):
    products = jnp.einsum('sfa,sfb->fab', home_spec.astype(jnp.float32), away_spec.astype(jnp.float32))
    bin_count = home_spec.shape[1]
    quarters = products.reshape(bin_count, 2, SB, 2, SB)
    real_part = quarters[:, 0, :, 0, :] + quarters[:, 1, :, 1, :]
    imag_part = quarters[:, 1, :, 0, :] - quarters[:, 0, :, 1, :]
    return jnp.stack([real_part, imag_part], 0).reshape(2, bin_count, SB * SB) / seg_total

def reference(raw_counts, seg_valid):
    stations_valid = seg_valid.reshape(SEGS, NBLK, SB)

    def one_block(block_id):
        samples = lax.dynamic_index_in_dim(raw_counts, block_id, 1, keepdims=False)
        validity = lax.dynamic_index_in_dim(stations_valid, block_id, 1, keepdims=False)
        history = jnp.zeros((HIST, DECIM * SB), raw_counts.dtype)
        return whiten(decimate(samples, history), validity)
    spectra = lax.map(one_block, jnp.arange(NBLK, dtype=jnp.int32))
    rounds_out = []
    for offset in range(1, ROUNDS + 1):

        def one_pair(block_id):
            partner_id = ((block_id - offset) % NBLK).astype(jnp.int32)
            home_spec = lax.dynamic_index_in_dim(spectra, block_id, 0, keepdims=False)
            away_spec = lax.dynamic_index_in_dim(spectra, partner_id, 0, keepdims=False)
            return cross_block(home_spec, away_spec, SEGS)
        rounds_out.append(lax.map(one_pair, jnp.arange(NBLK, dtype=jnp.int32)))
    return jnp.stack(rounds_out, 0)
```

```python
import functools
import math

import jax
import jax.numpy as jnp
import numpy as np
from jax import lax
from jax.experimental import pallas as pl
from jax.experimental.pallas import tpu as pltpu
from jax.sharding import PartitionSpec as P

SB = 64
LSEG = 600
NF = 320
DECIM = 10
TAPS = 64
SMOOTH = 33
ROUNDS = 2
HIST = 7

EPSILON = 1e-06
LANES = 128
SUB = 8
HALF = 304
PACKED = HALF + 16
BF16 = jnp.bfloat16
F32 = jnp.float32


def filter_coeffs():
    position = np.arange(TAPS, dtype=np.float64)
    centre = 0.5 * (TAPS - 1)
    cutoff = 0.4 / DECIM
    shaped = np.sinc(2.0 * cutoff * (position - centre))
    window = 0.54 - 0.46 * np.cos(2.0 * math.pi * position / (TAPS - 1))
    return 2.0 * cutoff * shaped * window


def tap_matrix():
    coeffs = filter_coeffs()
    weights = np.zeros((DECIM, HIST + 1))
    for p in range(DECIM):
        for o in range(HIST + 1):
            t = DECIM * o - p
            if 0 <= t < TAPS:
                weights[p, o] = coeffs[t]
    full = np.kron(weights, np.eye(SB)).astype(np.float32)
    high = full.astype(BF16)
    low = (full - high.astype(np.float32)).astype(BF16)
    return high, low


def window_of(first, count):
    width = count + SMOOTH - 1
    start = min(max(first - SMOOTH // 2, 0), NF - width)
    own = list(range(first, first + count))
    return own, [f for f in range(start, start + width) if f not in set(own)]


def tables(chunks):
    count = NF // chunks
    position = np.arange(2 * HALF)
    transforms, smoothers = [], []
    for chunk in range(chunks):
        own, others = window_of(chunk * count, count)
        rows = [(f, c) for g in range(0, count, SUB) for c in range(2) for f in own[g : g + SUB]]
        rows += [(f, c) for c in range(2) for f in others]
        bins = np.array([f for f, _ in rows])
        comps = np.array([c for _, c in rows])
        radians = ((bins[:, None] + 1) * position[None, :] % (2 * LSEG)) * (math.pi / LSEG)
        table = np.where(comps[:, None] == 0, np.cos(radians), -np.sin(radians))
        transforms.append(np.where(position[None, :] < LSEG, table, 0.0).astype(BF16))
        low = np.clip(bins[: 2 * count] - SMOOTH // 2, 0, NF - SMOOTH)
        inside = (bins[None, :] >= low[:, None]) & (bins[None, :] < low[:, None] + SMOOTH)
        smoothers.append(inside.astype(BF16))
    return np.stack(transforms), np.stack(smoothers)


def low_lanes(shape):
    return lax.broadcasted_iota(jnp.int32, shape, len(shape) - 1) % LANES < SB


def swap(value):
    return pltpu.roll(value, SB, 1)


def decimate_kernel(x_ref, valid_ref, high_ref, low_ref, out_ref, y_ref, e_ref):
    rows = x_ref.shape[0]
    x = x_ref[...]
    y_ref[0:16, :] = jnp.zeros((16, y_ref.shape[1]), F32)
    y_ref[16 + rows :, :] = jnp.zeros((y_ref.shape[0] - 16 - rows, y_ref.shape[1]), F32)
    y_ref[16 : 16 + rows, :] = jnp.dot(x, high_ref[...], preferred_element_type=F32) + jnp.dot(
        x, low_ref[...], preferred_element_type=F32
    )
    total = y_ref[8 : 8 + 616, 0:LANES]
    for j in range(1, (HIST + 1) // 2):
        total = total + y_ref[8 - 2 * j : 8 - 2 * j + 616, j * LANES : (j + 1) * LANES]
    e_ref[...] = total
    first = e_ref[8 : 8 + HALF, :] + swap(e_ref[7 : 7 + HALF, :])
    second = swap(e_ref[8 + HALF : 8 + 2 * HALF, :]) + e_ref[7 + HALF : 7 + 2 * HALF, :]
    value = jnp.where(low_lanes((HALF, LANES)), first, second)
    rounded = value.astype(BF16)
    out_ref[0:HALF, :] = rounded
    rest = value - rounded.astype(F32)
    ends = jnp.where(low_lanes((SUB, LANES)), rest[0:SUB], rest[HALF - SUB : HALF])
    valid = jnp.broadcast_to(valid_ref[...], (SUB, LANES))
    out_ref[HALF:PACKED, :] = jnp.concatenate([ends, valid], 0).astype(BF16)


def whiten_kernel(sizes, *refs):
    n_win, n_bin = sizes
    count = n_win * n_bin
    parts, (table_ref, smooth_ref, out_ref, q_ref) = refs[:count], refs[count:]
    my_win, my_bin = lax.axis_index("win"), lax.axis_index("bin")
    lanes8 = low_lanes((SUB, LANES))
    heads, tails, valids = [], [], []
    for part in parts:
        extra = part[HALF:PACKED, :].astype(F32)
        heads.append(part[0:16, :].astype(F32)[0:SUB] + extra[0:SUB])
        tails.append(swap(part[HALF - 16 : HALF, :].astype(F32)[SUB:] + extra[0:SUB]))
        valids.append(extra[SUB : SUB + 1])
    starts = []
    for d in range(n_win):
        for e in range(n_bin):
            win = lax.rem(my_win - d + n_win, n_win)
            core = lax.rem(my_bin - e + n_bin, n_bin)
            after = (e + 1) % n_bin
            same = tails[d * n_bin + after]
            other = tails[(d + 1) % n_win * n_bin + after]
            first = core == 0
            use_same = jnp.where(first, 0.0, 1.0).astype(F32)
            use_other = jnp.where(jnp.logical_and(first, win != 0), 1.0, 0.0).astype(F32)
            starts.append(heads[d * n_bin + e] + same * use_same + other * use_other)
    lanes = low_lanes((HALF, LANES))
    scales = []
    for q in range(count // 2):
        a = parts[2 * q][0:HALF, :].astype(F32)
        b = parts[2 * q + 1][0:HALF, :].astype(F32)
        column = slice(q * LANES, (q + 1) * LANES)
        early = jnp.where(lanes, a, swap(b))
        late = jnp.where(lanes, swap(a), b)
        begin = jnp.where(lanes8, starts[2 * q], swap(starts[2 * q + 1]))
        q_ref[0:HALF, column] = jnp.concatenate([begin, early[SUB:]], 0).astype(BF16)
        q_ref[HALF:, column] = late.astype(BF16)
        scales.append(jnp.where(low_lanes((1, LANES)), valids[2 * q], valids[2 * q + 1]))
    valid = jnp.concatenate(scales, 1)
    spectra = jnp.dot(table_ref[...], q_ref[...], preferred_element_type=F32)
    square = spectra * spectra
    square_high = square.astype(BF16)
    square_low = (square - square_high.astype(F32)).astype(BF16)
    smooth = smooth_ref[...]
    energy = jnp.dot(smooth, square_high, preferred_element_type=F32) + jnp.dot(
        smooth, square_low, preferred_element_type=F32
    )
    scale = valid * lax.rsqrt(energy * (1.0 / (2.0 * SMOOTH)) + EPSILON)
    out_ref[...] = (spectra[0 : out_ref.shape[0]] * scale).astype(BF16)


def spread(tile):
    low = low_lanes((SUB, LANES))
    zero = jnp.zeros((SUB, LANES), F32)
    tiles = []
    for q in range(tile.shape[1] // LANES):
        x = tile[:, q * LANES : (q + 1) * LANES]
        r = swap(x)
        tiles.append(
            [jnp.where(low, x, zero), jnp.where(low, zero, r), jnp.where(low, r, zero), jnp.where(low, zero, x)]
        )
    return tiles


def home_kernel(home_ref, out_ref):
    rows, depth = out_ref.shape[1], out_ref.shape[2]
    row = lax.broadcasted_iota(jnp.int32, (rows, LANES), 0)
    lane = lax.broadcasted_iota(jnp.int32, (rows, LANES), 1)
    pick = jnp.where(lane % SB == 2 * (row // SUB) + lane // SB, 1.0, 0.0).astype(BF16)
    row = lax.broadcasted_iota(jnp.int32, (rows, depth), 0)
    lane = lax.broadcasted_iota(jnp.int32, (rows, depth), 1)
    diagonal = row % SUB == lane % SUB
    for g in range(out_ref.shape[0]):
        values = home_ref[16 * g : 16 * g + 16, :].astype(F32)
        real, imag = spread(values[0:SUB]), spread(values[SUB:])
        stack = []
        for q in range(len(real)):
            stack += real[q] + imag[q]
        block = jnp.concatenate(stack, 0).astype(BF16)
        turned = lax.dot_general(pick, block, (((1,), (1,)), ((), ())), preferred_element_type=F32)
        out_ref[g] = jnp.where(diagonal, turned, 0.0).astype(BF16)


def cross_kernel(factor, home_ref, away_ref, *refs):
    out_ref = refs[-1]
    groups = home_ref.shape[0]
    for g in range(groups):
        values = away_ref[16 * g : 16 * g + 16, :].astype(F32)
        real, imag = spread(values[0:SUB]), spread(values[SUB:])
        left, right = [], []
        for q in range(len(real)):
            left += real[q] + imag[q]
            right += [-t for t in imag[q]] + real[q]
        block = jnp.concatenate([jnp.concatenate(left, 0), jnp.concatenate(right, 0)], 1).astype(BF16)
        product = jnp.dot(home_ref[g], block, preferred_element_type=F32) * factor
        for t in range(SB // 2):
            at = slice(t * LANES, (t + 1) * LANES)
            for c in range(2):
                out_ref[0, 0, c, SUB * g : SUB * g + SUB, at] = product[
                    SUB * t : SUB * t + SUB, c * LANES : (c + 1) * LANES
                ]


def shifted(value, axis, steps):
    size = lax.axis_size(axis)
    return lax.ppermute(value, axis, [(i, (i + steps) % size) for i in range(size)])


def cost(flops, moved):
    return pl.CostEstimate(flops=int(flops), bytes_accessed=int(moved), transcendentals=0)


def whole(*shape):
    return pl.BlockSpec(shape, lambda *_: (0,) * len(shape))


def per_device(raw_counts, seg_valid):
    n_win, n_bin = lax.axis_size("win"), lax.axis_size("bin")
    segs = n_win * n_bin
    samples = raw_counts[:, 0, :]
    rows = samples.shape[0]
    assert rows == LSEG and segs % 2 == 0 and NF % (SUB * segs) == 0
    valid = jnp.concatenate([seg_valid, seg_valid], 1).astype(F32)
    high, low = (jnp.asarray(t) for t in tap_matrix())
    packed = pl.pallas_call(
        decimate_kernel,
        out_shape=jax.ShapeDtypeStruct((PACKED, LANES), BF16),
        scratch_shapes=[pltpu.VMEM((632, high.shape[1]), F32), pltpu.VMEM((616, LANES), F32)],
        cost_estimate=cost(4 * rows * high.size, 2 * (samples.size + 2 * high.size)),
        name="decimate",
    )(samples, valid, high, low)

    mine = [packed] + [shifted(packed, "win", d) for d in range(1, n_win)]
    parts = []
    for value in mine:
        parts += [value] + [shifted(value, "bin", e) for e in range(1, n_bin)]

    transforms, smoothers = tables(segs)
    chunk = lax.axis_index(("win", "bin"))
    transform = lax.dynamic_index_in_dim(jnp.asarray(transforms), chunk, 0, keepdims=False)
    smoother = lax.dynamic_index_in_dim(jnp.asarray(smoothers), chunk, 0, keepdims=False)
    bins = NF // segs
    groups = bins // SUB
    width = segs * SB
    home = pl.pallas_call(
        functools.partial(whiten_kernel, (n_win, n_bin)),
        out_shape=jax.ShapeDtypeStruct((2 * bins, width), BF16),
        scratch_shapes=[pltpu.VMEM((2 * HALF, width), BF16)],
        cost_estimate=cost(2 * transform.size * width, 2 * (transform.size + 3 * bins * width)),
        name="whiten",
    )(*parts, transform, smoother)

    aways = [shifted(home, "blk", offset) for offset in range(1, ROUNDS + 1)]
    depth = segs * 4 * SUB
    tall = SB // 2 * SUB
    turned = pl.pallas_call(
        home_kernel,
        out_shape=jax.ShapeDtypeStruct((groups, tall, depth), BF16),
        cost_estimate=cost(2 * groups * tall * depth * LANES, 2 * groups * tall * depth),
        name="home",
    )(home)

    step = 2 if groups % 2 == 0 else 1
    stacks = None
    for offset in range(ROUNDS):
        extra = [] if stacks is None else [stacks]
        stacks = pl.pallas_call(
            functools.partial(cross_kernel, 1.0 / segs),
            out_shape=jax.ShapeDtypeStruct((ROUNDS, 1, 2, bins, SB * SB), F32),
            grid=(groups // step,),
            in_specs=[
                pl.BlockSpec((step, tall, depth), lambda g: (g, 0, 0)),
                pl.BlockSpec((16 * step, width), lambda g: (g, 0)),
            ]
            + [pl.BlockSpec(memory_space=pl.ANY)] * len(extra),
            out_specs=pl.BlockSpec(
                (1, 1, 2, SUB * step, SB * SB), functools.partial(lambda r, g: (r, 0, 0, g, 0), offset)
            ),
            input_output_aliases={2: 0} if extra else {},
            cost_estimate=cost(4 * groups * tall * depth * LANES, 8 * bins * SB * SB),
            name="cross",
        )(turned, aways[offset], *extra)
    return stacks


def solution(mesh):
    in_specs = (P(("win", "bin"), ("parts", "blk"), None), P(("win", "bin"), ("parts", "blk")))
    out_specs = P(None, ("parts", "blk"), None, ("win", "bin"), None)
    return jax.shard_map(
        per_device, mesh=mesh, in_specs=in_specs, out_specs=out_specs, check_vma=False
    )
```

```python
import functools
import math

import jax
import jax.numpy as jnp
import numpy as np
from jax import lax
from jax.experimental import pallas as pl
from jax.experimental.pallas import tpu as pltpu
from jax.sharding import PartitionSpec as P

SB = 64
LSEG = 600
NF = 320
DECIM = 10
TAPS = 64
SMOOTH = 33
ROUNDS = 2
HIST = 7

EPSILON = 1e-06
LANES = 128
SUB = 8
HALF = 304
PACKED = HALF + 16
BF16 = jnp.bfloat16
F32 = jnp.float32


def filter_coeffs():
    position = np.arange(TAPS, dtype=np.float64)
    centre = 0.5 * (TAPS - 1)
    cutoff = 0.4 / DECIM
    shaped = np.sinc(2.0 * cutoff * (position - centre))
    window = 0.54 - 0.46 * np.cos(2.0 * math.pi * position / (TAPS - 1))
    return 2.0 * cutoff * shaped * window


def taps():
    coeffs = filter_coeffs()
    weights = np.zeros((DECIM, HIST + 1), np.float32)
    for p in range(DECIM):
        for o in range(HIST + 1):
            t = DECIM * o - p
            if 0 <= t < TAPS:
                weights[p, o] = coeffs[t]
    high = weights.astype(BF16).astype(np.float32)
    low = (weights - high).astype(BF16).astype(np.float32)
    return high, low


def window_of(first, count):
    width = count + SMOOTH - 1
    start = min(max(first - SMOOTH // 2, 0), NF - width)
    own = list(range(first, first + count))
    return own, [f for f in range(start, start + width) if f not in set(own)]


def tables(chunks):
    count = NF // chunks
    position = np.arange(2 * HALF)
    transforms, smoothers = [], []
    for chunk in range(chunks):
        own, others = window_of(chunk * count, count)
        rows = [(f, c) for g in range(0, count, SUB) for c in range(2) for f in own[g : g + SUB]]
        rows += [(f, c) for c in range(2) for f in others]
        bins = np.array([f for f, _ in rows])
        comps = np.array([c for _, c in rows])
        radians = ((bins[:, None] + 1) * position[None, :] % (2 * LSEG)) * (math.pi / LSEG)
        table = np.where(comps[:, None] == 0, np.cos(radians), -np.sin(radians))
        transforms.append(np.where(position[None, :] < LSEG, table, 0.0).astype(BF16))
        low = np.clip(bins[: 2 * count] - SMOOTH // 2, 0, NF - SMOOTH)
        inside = (bins[None, :] >= low[:, None]) & (bins[None, :] < low[:, None] + SMOOTH)
        smoothers.append(inside.astype(BF16))
    return np.stack(transforms), np.stack(smoothers)


def low_lanes(shape):
    return lax.broadcasted_iota(jnp.int32, shape, len(shape) - 1) % LANES < SB


def swap(value):
    return pltpu.roll(value, SB, 1)


def decimate_kernel(
    x_hbm, valid_hbm, table_hbm, smooth_hbm, out_ref, table_ref, smooth_ref, x_ref, valid_ref, tap_ref, y_ref, e_ref, sem
):
    rows = x_ref.shape[0]
    chunk = lax.axis_index("win") * lax.axis_size("bin") + lax.axis_index("bin")
    copies = [
        pltpu.make_async_copy(x_hbm, x_ref, sem.at[0]),
        pltpu.make_async_copy(valid_hbm, valid_ref, sem.at[1]),
        pltpu.make_async_copy(table_hbm.at[chunk], table_ref, sem.at[2]),
        pltpu.make_async_copy(smooth_hbm.at[chunk], smooth_ref, sem.at[3]),
    ]
    for copy in copies:
        copy.start()
    row = lax.broadcasted_iota(jnp.int32, (SB, LANES), 0)
    lane = lax.broadcasted_iota(jnp.int32, (SB, LANES), 1)
    same, low = lane % SB == row, lane < SB
    zero = jnp.zeros((SB, LANES), F32)
    for part, values in enumerate(taps()):
        for p in range(DECIM):
            for j in range((HIST + 1) // 2):
                pair = jnp.where(low, float(values[p, 2 * j]), float(values[p, 2 * j + 1]))
                tap_ref[part, p * SB : (p + 1) * SB, j * LANES : (j + 1) * LANES] = jnp.where(same, pair, zero).astype(BF16)
    y_ref[0:16, :] = jnp.zeros((16, y_ref.shape[1]), F32)
    y_ref[16 + rows :, :] = jnp.zeros((y_ref.shape[0] - 16 - rows, y_ref.shape[1]), F32)
    copies[0].wait()
    x = x_ref[...]
    y_ref[16 : 16 + rows, :] = jnp.dot(x, tap_ref[0], preferred_element_type=F32) + jnp.dot(
        x, tap_ref[1], preferred_element_type=F32
    )
    total = y_ref[8 : 8 + 616, 0:LANES]
    for j in range(1, (HIST + 1) // 2):
        total = total + y_ref[8 - 2 * j : 8 - 2 * j + 616, j * LANES : (j + 1) * LANES]
    e_ref[...] = total
    first = e_ref[8 : 8 + HALF, :] + swap(e_ref[7 : 7 + HALF, :])
    second = swap(e_ref[8 + HALF : 8 + 2 * HALF, :]) + e_ref[7 + HALF : 7 + 2 * HALF, :]
    value = jnp.where(low_lanes((HALF, LANES)), first, second)
    rounded = value.astype(BF16)
    out_ref[0:HALF, :] = rounded
    rest = value - rounded.astype(F32)
    ends = jnp.where(low_lanes((SUB, LANES)), rest[0:SUB], rest[HALF - SUB : HALF])
    copies[1].wait()
    valid = valid_ref[...].astype(F32)
    valid = jnp.broadcast_to(jnp.concatenate([valid, valid], 1), (SUB, LANES))
    out_ref[HALF:PACKED, :] = jnp.concatenate([ends, valid], 0).astype(BF16)
    copies[2].wait()
    copies[3].wait()


def whiten_kernel(sizes, *refs):
    n_win, n_bin = sizes
    count = n_win * n_bin
    parts, (table_ref, smooth_ref, out_ref, q_ref) = refs[:count], refs[count:]
    my_win, my_bin = lax.axis_index("win"), lax.axis_index("bin")
    lanes8 = low_lanes((SUB, LANES))
    heads, tails, valids = [], [], []
    for part in parts:
        extra = part[HALF:PACKED, :].astype(F32)
        heads.append(part[0:16, :].astype(F32)[0:SUB] + extra[0:SUB])
        tails.append(swap(part[HALF - 16 : HALF, :].astype(F32)[SUB:] + extra[0:SUB]))
        valids.append(extra[SUB : SUB + 1])
    starts = []
    for d in range(n_win):
        for e in range(n_bin):
            win = lax.rem(my_win - d + n_win, n_win)
            core = lax.rem(my_bin - e + n_bin, n_bin)
            after = (e + 1) % n_bin
            same = tails[d * n_bin + after]
            other = tails[(d + 1) % n_win * n_bin + after]
            first = core == 0
            use_same = jnp.where(first, 0.0, 1.0).astype(F32)
            use_other = jnp.where(jnp.logical_and(first, win != 0), 1.0, 0.0).astype(F32)
            starts.append(heads[d * n_bin + e] + same * use_same + other * use_other)
    lanes = low_lanes((HALF, LANES))
    scales = []
    for q in range(count // 2):
        a = parts[2 * q][0:HALF, :].astype(F32)
        b = parts[2 * q + 1][0:HALF, :].astype(F32)
        column = slice(q * LANES, (q + 1) * LANES)
        early = jnp.where(lanes, a, swap(b))
        late = jnp.where(lanes, swap(a), b)
        begin = jnp.where(lanes8, starts[2 * q], swap(starts[2 * q + 1]))
        q_ref[0:HALF, column] = jnp.concatenate([begin, early[SUB:]], 0).astype(BF16)
        q_ref[HALF:, column] = late.astype(BF16)
        scales.append(jnp.where(low_lanes((1, LANES)), valids[2 * q], valids[2 * q + 1]))
    valid = jnp.concatenate(scales, 1)
    spectra = jnp.dot(table_ref[...], q_ref[...], preferred_element_type=F32)
    square = spectra * spectra
    square_high = square.astype(BF16)
    square_low = (square - square_high.astype(F32)).astype(BF16)
    smooth = smooth_ref[...]
    energy = jnp.dot(smooth, square_high, preferred_element_type=F32) + jnp.dot(
        smooth, square_low, preferred_element_type=F32
    )
    scale = valid * lax.rsqrt(energy * (1.0 / (2.0 * SMOOTH)) + EPSILON)
    out_ref[...] = (spectra[0 : out_ref.shape[0]] * scale).astype(BF16)


def spread(tile):
    low = low_lanes((SUB, LANES))
    zero = jnp.zeros((SUB, LANES), F32)
    tiles = []
    for q in range(tile.shape[1] // LANES):
        x = tile[:, q * LANES : (q + 1) * LANES]
        r = swap(x)
        tiles.append(
            [jnp.where(low, x, zero), jnp.where(low, zero, r), jnp.where(low, r, zero), jnp.where(low, zero, x)]
        )
    return tiles


def home_kernel(home_ref, out_ref):
    rows, depth = out_ref.shape[1], out_ref.shape[2]
    row = lax.broadcasted_iota(jnp.int32, (rows, LANES), 0)
    lane = lax.broadcasted_iota(jnp.int32, (rows, LANES), 1)
    pick = jnp.where(lane % SB == 2 * (row // SUB) + lane // SB, 1.0, 0.0).astype(BF16)
    row = lax.broadcasted_iota(jnp.int32, (rows, depth), 0)
    lane = lax.broadcasted_iota(jnp.int32, (rows, depth), 1)
    diagonal = row % SUB == lane % SUB
    for g in range(out_ref.shape[0]):
        values = home_ref[16 * g : 16 * g + 16, :].astype(F32)
        real, imag = spread(values[0:SUB]), spread(values[SUB:])
        stack = []
        for q in range(len(real)):
            stack += real[q] + imag[q]
        block = jnp.concatenate(stack, 0).astype(BF16)
        turned = lax.dot_general(pick, block, (((1,), (1,)), ((), ())), preferred_element_type=F32)
        out_ref[g] = jnp.where(diagonal, turned, 0.0).astype(BF16)


def cross_kernel(offset, factor, home_ref, away_ref, *refs):
    out_hbm, out_ref, sem = refs[-3:]
    groups = home_ref.shape[0]
    copies = []
    for g in range(groups):
        values = away_ref[16 * g : 16 * g + 16, :].astype(F32)
        real, imag = spread(values[0:SUB]), spread(values[SUB:])
        left, right = [], []
        for q in range(len(real)):
            left += real[q] + imag[q]
            right += [-t for t in imag[q]] + real[q]
        block = jnp.concatenate([jnp.concatenate(left, 0), jnp.concatenate(right, 0)], 1).astype(BF16)
        product = jnp.dot(home_ref[g], block, preferred_element_type=F32) * factor
        at = pl.ds(SUB * g, SUB)
        for c in range(2):
            for t in range(SB // 2):
                out_ref[c, SUB * g : SUB * g + SUB, t * LANES : (t + 1) * LANES] = product[
                    SUB * t : SUB * t + SUB, c * LANES : (c + 1) * LANES
                ]
            copies.append(pltpu.make_async_copy(out_ref.at[c, at], out_hbm.at[offset, 0, c, at], sem.at[2 * g + c]))
            copies[-1].start()
    for copy in copies:
        copy.wait()


def shifted(value, axis, steps):
    size = lax.axis_size(axis)
    return lax.ppermute(value, axis, [(i, (i + steps) % size) for i in range(size)])


def cost(flops, moved):
    return pl.CostEstimate(flops=int(flops), bytes_accessed=int(moved), transcendentals=0)


def room(limit):
    return pltpu.CompilerParams(vmem_limit_bytes=limit)


VMEM = pl.BlockSpec(memory_space=pltpu.VMEM)
HBM = pl.BlockSpec(memory_space=pl.ANY)


def per_device(raw_counts, seg_valid):
    n_win, n_bin = lax.axis_size("win"), lax.axis_size("bin")
    segs = n_win * n_bin
    samples = raw_counts[:, 0, :]
    rows = samples.shape[0]
    assert rows == LSEG and segs % 2 == 0 and NF % (SUB * segs) == 0
    transforms, smoothers = tables(segs)
    wide = (HIST + 1) * SB
    packed, transform, smoother = pl.pallas_call(
        decimate_kernel,
        out_shape=(
            jax.ShapeDtypeStruct((PACKED, LANES), BF16),
            jax.ShapeDtypeStruct(transforms.shape[1:], BF16),
            jax.ShapeDtypeStruct(smoothers.shape[1:], BF16),
        ),
        in_specs=[pl.BlockSpec(memory_space=pltpu.HBM)] * 4,
        out_specs=(VMEM,) * 3,
        scratch_shapes=[
            pltpu.VMEM(samples.shape, BF16),
            pltpu.VMEM(seg_valid.shape, jnp.int32),
            pltpu.VMEM((2, DECIM * SB, wide), BF16),
            pltpu.VMEM((632, wide), F32),
            pltpu.VMEM((616, LANES), F32),
            pltpu.SemaphoreType.DMA((4,)),
        ],
        cost_estimate=cost(4 * rows * DECIM * SB * wide, 2 * samples.size),
        compiler_params=room(16 << 20),
        name="decimate",
    )(*(pltpu.with_memory_space_constraint(v, pltpu.HBM) for v in (samples, seg_valid, jnp.asarray(transforms), jnp.asarray(smoothers))))

    mine = [packed] + [shifted(packed, "win", d) for d in range(1, n_win)]
    parts = []
    for value in mine:
        parts += [value] + [shifted(value, "bin", e) for e in range(1, n_bin)]

    bins = NF // segs
    groups = bins // SUB
    width = segs * SB
    home = pl.pallas_call(
        functools.partial(whiten_kernel, (n_win, n_bin)),
        out_shape=jax.ShapeDtypeStruct((2 * bins, width), BF16),
        in_specs=[VMEM] * (segs + 2),
        out_specs=VMEM,
        scratch_shapes=[pltpu.VMEM((2 * HALF, width), BF16)],
        cost_estimate=cost(2 * transform.size * width, 2 * (transform.size + 3 * bins * width)),
        compiler_params=room(6 << 20),
        name="whiten",
    )(*parts, transform, smoother)

    aways = [shifted(home, "blk", offset) for offset in range(1, ROUNDS + 1)]
    depth = segs * 4 * SUB
    tall = SB // 2 * SUB
    turned = pl.pallas_call(
        home_kernel,
        out_shape=jax.ShapeDtypeStruct((groups, tall, depth), BF16),
        in_specs=[VMEM],
        out_specs=VMEM,
        cost_estimate=cost(2 * groups * tall * depth * LANES, 2 * groups * tall * depth),
        compiler_params=room(6 << 20),
        name="home",
    )(home)

    stacks = None
    for offset in range(ROUNDS):
        extra = [] if stacks is None else [stacks]
        stacks = pl.pallas_call(
            functools.partial(cross_kernel, offset, 1.0 / segs),
            out_shape=jax.ShapeDtypeStruct((ROUNDS, 1, 2, bins, SB * SB), F32),
            in_specs=[VMEM] * 2 + [HBM] * len(extra),
            out_specs=HBM,
            scratch_shapes=[pltpu.VMEM((2, bins, SB * SB), F32), pltpu.SemaphoreType.DMA((2 * groups,))],
            input_output_aliases={2: 0} if extra else {},
            cost_estimate=cost(4 * groups * tall * depth * LANES, 8 * bins * SB * SB),
            compiler_params=room(8 << 20),
            name="cross",
        )(turned, aways[offset], *extra)
    return stacks


def solution(mesh):
    in_specs = (P(("win", "bin"), ("parts", "blk"), None), P(("win", "bin"), ("parts", "blk")))
    out_specs = P(None, ("parts", "blk"), None, ("win", "bin"), None)
    return jax.shard_map(
        per_device, mesh=mesh, in_specs=in_specs, out_specs=out_specs, check_vma=False
    )
```

```python
import functools
import math

import jax
import jax.numpy as jnp
import numpy as np
from jax import lax
from jax.experimental import pallas as pl
from jax.experimental.pallas import tpu as pltpu
from jax.sharding import PartitionSpec as P

SB = 64
LSEG = 600
NF = 320
DECIM = 10
TAPS = 64
SMOOTH = 33
ROUNDS = 2
HIST = 7

EPSILON = 1e-06
LANES = 128
SUB = 8
HALF = 320
CHUNK = 32
BACK = 16
BF16 = jnp.bfloat16
F32 = jnp.float32


def filter_coeffs():
    position = np.arange(TAPS, dtype=np.float64)
    centre = 0.5 * (TAPS - 1)
    cutoff = 0.4 / DECIM
    shaped = np.sinc(2.0 * cutoff * (position - centre))
    window = 0.54 - 0.46 * np.cos(2.0 * math.pi * position / (TAPS - 1))
    return 2.0 * cutoff * shaped * window


def taps():
    coeffs = filter_coeffs()
    weights = np.zeros((DECIM, HIST + 1), np.float32)
    for p in range(DECIM):
        for o in range(HIST + 1):
            t = DECIM * o - p
            if 0 <= t < TAPS:
                weights[p, o] = coeffs[t]
    high = weights.astype(BF16).astype(np.float32)
    low = (weights - high).astype(BF16).astype(np.float32)
    return high, low


def tap_matrix():
    out = np.zeros((2, 2, CHUNK, DECIM // 2, BACK + CHUNK), np.float32)
    for part, values in enumerate(taps()):
        for p in range(DECIM):
            for o in range(HIST + 1):
                for n in range(CHUNK):
                    out[part, p % 2, n, p // 2, BACK + n - o] = values[p, o]
    return out.reshape(4 * CHUNK, DECIM // 2 * (BACK + CHUNK)).astype(BF16)


def window(count):
    return count + SMOOTH - 1


def phases(bins, samples):
    return ((bins[:, None] + 1) * samples[None, :] % (2 * LSEG)) * (math.pi / LSEG)


def transform_table():
    samples = np.arange(2 * HALF)
    radians = phases(np.arange(NF), samples)
    inside = samples[None, :] < LSEG
    parts = [np.where(inside, np.cos(radians), 0.0), np.where(inside, -np.sin(radians), 0.0)]
    return np.concatenate(parts, 1).astype(BF16)


def window_tables(chunks):
    count = NF // chunks
    width = window(count)
    assert width <= LANES
    out = np.zeros((chunks, width + count, LANES), np.float32)
    for chunk in range(chunks):
        start = min(max(chunk * count - SMOOTH // 2, 0), NF - width)
        bins = np.arange(start, start + width)
        radians = phases(bins, np.arange(SUB))
        first = np.concatenate([np.cos(radians), -np.sin(radians)], 1)
        out[chunk, :width, : 4 * SUB] = np.concatenate([first, first], 1)
        own = np.arange(chunk * count, (chunk + 1) * count)
        low = np.clip(own - SMOOTH // 2, 0, NF - SMOOTH)
        out[chunk, width:, :width] = (bins[None, :] >= low[:, None]) & (bins[None, :] < low[:, None] + SMOOTH)
    return out.astype(BF16)


def low_lanes(shape):
    return lax.broadcasted_iota(jnp.int32, shape, len(shape) - 1) % LANES < SB


def swap(value):
    return pltpu.roll(value, SB, 1)


def spread(tile):
    low = low_lanes(tile.shape)
    zero = jnp.zeros(tile.shape, F32)
    other = swap(tile)
    return [
        jnp.where(low, tile, zero),
        jnp.where(low, zero, other),
        jnp.where(low, other, zero),
        jnp.where(low, zero, tile),
    ]


def window_start(chunk, count):
    return jnp.clip(chunk * count - SMOOTH // 2, 0, NF - window(count))


def segment_kernel(sizes, x_hbm, taps_hbm, valid_hbm, table_hbm, windows_hbm, *refs):
    n_win, n_bin = sizes
    segs = n_win * n_bin
    outs, (windows_ref, x_ref, taps_ref, valid_ref, table_ref, s_ref, sem) = refs[:segs], refs[segs:]
    rows = x_hbm.shape[0]
    my_win, my_bin = lax.axis_index("win"), lax.axis_index("bin")
    x_ref[0:BACK, :] = jnp.zeros((BACK, x_ref.shape[1]), BF16)
    x_ref[BACK + rows :, :] = jnp.zeros((x_ref.shape[0] - BACK - rows, x_ref.shape[1]), BF16)
    copies = [
        pltpu.make_async_copy(x_hbm, x_ref.at[pl.ds(BACK, rows)], sem.at[0]),
        pltpu.make_async_copy(taps_hbm, taps_ref, sem.at[1]),
        pltpu.make_async_copy(valid_hbm, valid_ref, sem.at[2]),
        pltpu.make_async_copy(table_hbm, table_ref, sem.at[3]),
        pltpu.make_async_copy(windows_hbm.at[my_win * n_bin + my_bin], windows_ref, sem.at[4]),
    ]
    for copy in copies:
        copy.start()
    copies[1].wait()
    copies[0].wait()
    matrix = taps_ref[...]
    low = low_lanes((CHUNK, LANES))
    chunks = []
    for c in range(HALF // CHUNK):
        sides = []
        for start in (c * CHUNK, c * CHUNK + HALF):
            window_rows = x_ref[start : start + BACK + CHUNK, :]
            sides.append(
                jnp.concatenate([window_rows[:, t * LANES : (t + 1) * LANES] for t in range(DECIM // 2)], 0)
            )
        product = jnp.dot(matrix, jnp.concatenate(sides, 1), preferred_element_type=F32)
        product = product[0 : 2 * CHUNK] + product[2 * CHUNK :]
        even, odd = product[:CHUNK], product[CHUNK:]
        stay = jnp.where(low, even[:, :LANES], odd[:, LANES:])
        cross = jnp.where(low, even[:, LANES:], odd[:, :LANES])
        chunks.append(stay + swap(cross))
    value = jnp.concatenate(chunks, 0)
    low = low_lanes((HALF, LANES))
    zero = jnp.zeros((HALF, LANES), F32)
    other = swap(value)
    operand = jnp.concatenate(
        [
            jnp.where(low, value, zero).astype(BF16),
            jnp.where(low, other, zero).astype(BF16),
            jnp.where(low, zero, other).astype(BF16),
            jnp.where(low, zero, value).astype(BF16),
        ],
        0,
    )
    copies[3].wait()
    s_ref[...] = jnp.dot(table_ref[...], operand, preferred_element_type=F32)
    tail = swap(value[LSEG - HALF : LSEG - HALF + SUB])
    high_part = tail.astype(BF16).astype(F32)
    tail = jnp.where(low_lanes((SUB, LANES)), high_part, swap(tail - high_part))
    copies[2].wait()
    valid = valid_ref[...].astype(F32)
    valid = jnp.broadcast_to(jnp.concatenate([valid, valid], 1), (SUB, LANES))
    extra = jnp.concatenate([tail, valid], 0).astype(BF16)
    count = NF // segs
    width = window(count)
    for d in range(n_win):
        for e in range(n_bin):
            chunk = lax.rem(my_win + d, n_win) * n_bin + lax.rem(my_bin + e, n_bin)
            start = pl.multiple_of(window_start(chunk, count), SUB)
            out_ref = outs[d * n_bin + e]
            out_ref[0:16, :] = extra
            out_ref[16:, :] = s_ref[pl.ds(start, width), :].astype(BF16)
    copies[4].wait()


def whiten_kernel(sizes, *refs):
    n_win, n_bin = sizes
    segs = n_win * n_bin
    parts, (windows_ref, out_ref, s_ref) = refs[:segs], refs[segs:]
    my_win, my_bin = lax.axis_index("win"), lax.axis_index("bin")
    count = NF // segs
    width = window(count)
    chunk = my_win * n_bin + my_bin
    extras = [part[0:16, :].astype(F32) for part in parts]
    tails = []
    for d in range(n_win):
        for e in range(n_bin):
            win = lax.rem(my_win - d + n_win, n_win)
            core = lax.rem(my_bin - e + n_bin, n_bin)
            after = (e + 1) % n_bin
            first = core == 0
            use_same = jnp.where(first, 0.0, 1.0).astype(F32)
            use_other = jnp.where(jnp.logical_and(first, win != 0), 1.0, 0.0).astype(F32)
            same = extras[d * n_bin + after][0:SUB]
            other = extras[(d + 1) % n_win * n_bin + after][0:SUB]
            tails.append(jnp.concatenate(spread(same * use_same + other * use_other), 0).astype(BF16))
    spectra = jnp.dot(windows_ref[0:width, 0 : 4 * SUB], jnp.concatenate(tails, 1), preferred_element_type=F32)
    spectra = spectra + jnp.concatenate([part[16:, :].astype(F32) for part in parts], 1)
    s_ref[...] = spectra
    square = spectra * spectra
    square_high = square.astype(BF16)
    square_low = (square - square_high.astype(F32)).astype(BF16)
    smooth = windows_ref[width:, 0:width]
    energy = jnp.dot(smooth, square_high, preferred_element_type=F32) + jnp.dot(
        smooth, square_low, preferred_element_type=F32
    )
    own = pl.multiple_of(chunk * count - window_start(chunk, count), SUB)
    whites = []
    for s in range(segs):
        at = slice(s * LANES, (s + 1) * LANES)
        total = energy[:, at] + swap(energy[:, at])
        scale = extras[s][SUB : SUB + 1] * lax.rsqrt(total * (1.0 / (2.0 * SMOOTH)) + EPSILON)
        whites.append(s_ref[pl.ds(own, count), at] * scale)
    for g in range(count // SUB):
        tiles = [white[SUB * g : SUB * g + SUB] for white in whites]
        out_ref[SUB * segs * g : SUB * segs * (g + 1), :] = jnp.concatenate(tiles, 0).astype(BF16)


def operands(values):
    left, right = [], []
    for s in range(values.shape[0] // SUB):
        real_even, real_odd, imag_even, imag_odd = spread(values[SUB * s : SUB * s + SUB])
        left += [real_even, real_odd, imag_even, imag_odd]
        right += [-imag_even, -imag_odd, real_even, real_odd]
    return jnp.concatenate(left, 0), jnp.concatenate(right, 0)


def home_kernel(home_ref, out_ref):
    groups, rows, depth = out_ref.shape
    row = lax.broadcasted_iota(jnp.int32, (rows, LANES), 0)
    lane = lax.broadcasted_iota(jnp.int32, (rows, LANES), 1)
    pick = jnp.where(lane % SB == 2 * (row // SUB) + lane // SB, 1.0, 0.0).astype(BF16)
    row = lax.broadcasted_iota(jnp.int32, (rows, depth), 0)
    lane = lax.broadcasted_iota(jnp.int32, (rows, depth), 1)
    diagonal = row % SUB == lane % SUB
    size = home_ref.shape[0] // groups
    for g in range(groups):
        left, _ = operands(home_ref[size * g : size * (g + 1), :].astype(F32))
        turned = lax.dot_general(pick, left.astype(BF16), (((1,), (1,)), ((), ())), preferred_element_type=F32)
        out_ref[g] = jnp.where(diagonal, turned, 0.0).astype(BF16)


def cross_kernel(offset, factor, home_ref, away_ref, *refs):
    out_hbm, out_ref, sem = refs[-3:]
    groups = home_ref.shape[0]
    size = away_ref.shape[0] // groups
    copies = []
    for g in range(groups):
        block = jnp.concatenate(operands(away_ref[size * g : size * (g + 1), :].astype(F32)), 1).astype(BF16)
        product = jnp.dot(home_ref[g], block, preferred_element_type=F32) * factor
        at = pl.ds(SUB * g, SUB)
        for c in range(2):
            for t in range(SB // 2):
                out_ref[c, SUB * g : SUB * g + SUB, t * LANES : (t + 1) * LANES] = product[
                    SUB * t : SUB * t + SUB, c * LANES : (c + 1) * LANES
                ]
            copies.append(pltpu.make_async_copy(out_ref.at[c, at], out_hbm.at[offset, 0, c, at], sem.at[2 * g + c]))
            copies[-1].start()
    for copy in copies:
        copy.wait()


def shifted(value, axis, steps):
    size = lax.axis_size(axis)
    return lax.ppermute(value, axis, [(i, (i + steps) % size) for i in range(size)])


def cost(flops, moved):
    return pl.CostEstimate(flops=int(flops), bytes_accessed=int(moved), transcendentals=0)


def room(limit):
    return pltpu.CompilerParams(vmem_limit_bytes=limit)


VMEM = pl.BlockSpec(memory_space=pltpu.VMEM)
HBM = pl.BlockSpec(memory_space=pl.ANY)


def per_device(raw_counts, seg_valid):
    n_win, n_bin = lax.axis_size("win"), lax.axis_size("bin")
    segs = n_win * n_bin
    samples = raw_counts[:, 0, :]
    rows = samples.shape[0]
    assert rows == LSEG and NF % (SUB * segs) == 0
    bins = NF // segs
    groups = bins // SUB
    rows_sent = window(bins) + 16
    matrix, table, windows = (jnp.asarray(t) for t in (tap_matrix(), transform_table(), window_tables(segs)))
    *sent, own_window = pl.pallas_call(
        functools.partial(segment_kernel, (n_win, n_bin)),
        out_shape=(jax.ShapeDtypeStruct((rows_sent, LANES), BF16),) * segs
        + (jax.ShapeDtypeStruct(windows.shape[1:], BF16),),
        in_specs=[pl.BlockSpec(memory_space=pltpu.HBM)] * 5,
        out_specs=(VMEM,) * (segs + 1),
        scratch_shapes=[
            pltpu.VMEM((BACK + 2 * HALF, samples.shape[1]), BF16),
            pltpu.VMEM(matrix.shape, BF16),
            pltpu.VMEM(seg_valid.shape, jnp.int32),
            pltpu.VMEM(table.shape, BF16),
            pltpu.VMEM((NF, LANES), F32),
            pltpu.SemaphoreType.DMA((5,)),
        ],
        cost_estimate=cost(8 * samples.size * 2 * LANES, 2 * (samples.size + table.size)),
        compiler_params=room(16 << 20),
        name="segment",
    )(*(pltpu.with_memory_space_constraint(v, pltpu.HBM) for v in (samples, matrix, seg_valid, table, windows)))

    parts = [sent[0]] + [None] * (segs - 1)
    for d in reversed(range(n_win)):
        for e in range(n_bin):
            if d or e:
                route = [
                    (w * n_bin + c, (w + d) % n_win * n_bin + (c + e) % n_bin) for w in range(n_win) for c in range(n_bin)
                ]
                parts[d * n_bin + e] = lax.ppermute(sent[d * n_bin + e], ("win", "bin"), route)
    home = pl.pallas_call(
        functools.partial(whiten_kernel, (n_win, n_bin)),
        out_shape=jax.ShapeDtypeStruct((segs * bins, LANES), BF16),
        in_specs=[VMEM] * (segs + 1),
        out_specs=VMEM,
        scratch_shapes=[pltpu.VMEM((window(bins), segs * LANES), F32)],
        cost_estimate=cost(4 * bins * window(bins) * segs * LANES, 8 * segs * bins * LANES),
        compiler_params=room(6 << 20),
        name="whiten",
    )(*parts, own_window)

    aways = [shifted(home, "blk", offset) for offset in range(1, ROUNDS + 1)]
    depth = segs * 4 * SUB
    tall = SB // 2 * SUB
    turned = pl.pallas_call(
        home_kernel,
        out_shape=jax.ShapeDtypeStruct((groups, tall, depth), BF16),
        in_specs=[VMEM],
        out_specs=VMEM,
        cost_estimate=cost(2 * groups * tall * depth * LANES, 2 * groups * tall * depth),
        compiler_params=room(6 << 20),
        name="home",
    )(home)

    stacks = None
    for offset in range(ROUNDS):
        extra = [] if stacks is None else [stacks]
        stacks = pl.pallas_call(
            functools.partial(cross_kernel, offset, 1.0 / segs),
            out_shape=jax.ShapeDtypeStruct((ROUNDS, 1, 2, bins, SB * SB), F32),
            in_specs=[VMEM] * 2 + [HBM] * len(extra),
            out_specs=HBM,
            scratch_shapes=[pltpu.VMEM((2, bins, SB * SB), F32), pltpu.SemaphoreType.DMA((2 * groups,))],
            input_output_aliases={2: 0} if extra else {},
            cost_estimate=cost(4 * groups * tall * depth * LANES, 8 * bins * SB * SB),
            compiler_params=room(8 << 20),
            name="cross",
        )(turned, aways[offset], *extra)
    return stacks


def solution(mesh):
    in_specs = (P(("win", "bin"), ("parts", "blk"), None), P(("win", "bin"), ("parts", "blk")))
    out_specs = P(None, ("parts", "blk"), None, ("win", "bin"), None)
    return jax.shard_map(
        per_device, mesh=mesh, in_specs=in_specs, out_specs=out_specs, check_vma=False
    )
```

```python
import functools
import math

import jax
import jax.numpy as jnp
import numpy as np
from jax import lax
from jax.experimental import pallas as pl
from jax.experimental.pallas import tpu as pltpu
from jax.sharding import PartitionSpec as P

SB = 64
LSEG = 600
NF = 320
DECIM = 10
TAPS = 64
SMOOTH = 33
ROUNDS = 2
HIST = 7

EPSILON = 1e-06
LANES = 128
SUB = 8
HALF = 320
CHUNK = 32
BACK = 16
BF16 = jnp.bfloat16
F32 = jnp.float32


def filter_coeffs():
    position = np.arange(TAPS, dtype=np.float64)
    centre = 0.5 * (TAPS - 1)
    cutoff = 0.4 / DECIM
    shaped = np.sinc(2.0 * cutoff * (position - centre))
    window = 0.54 - 0.46 * np.cos(2.0 * math.pi * position / (TAPS - 1))
    return 2.0 * cutoff * shaped * window


def taps():
    coeffs = filter_coeffs()
    weights = np.zeros((DECIM, HIST + 1), np.float32)
    for p in range(DECIM):
        for o in range(HIST + 1):
            t = DECIM * o - p
            if 0 <= t < TAPS:
                weights[p, o] = coeffs[t]
    high = weights.astype(BF16).astype(np.float32)
    low = (weights - high).astype(BF16).astype(np.float32)
    return high, low


def tap_matrix():
    out = np.zeros((2, 2, CHUNK, DECIM // 2, BACK + CHUNK), np.float32)
    for part, values in enumerate(taps()):
        for p in range(DECIM):
            for o in range(HIST + 1):
                for n in range(CHUNK):
                    out[part, p % 2, n, p // 2, BACK + n - o] = values[p, o]
    return out.reshape(4 * CHUNK, DECIM // 2 * (BACK + CHUNK)).astype(BF16)


def window(count):
    return count + SMOOTH - 1


def phases(bins, samples):
    return ((bins[:, None] + 1) * samples[None, :] % (2 * LSEG)) * (math.pi / LSEG)


def transform_table():
    samples = np.arange(2 * HALF)
    radians = phases(np.arange(NF), samples)
    inside = samples[None, :] < LSEG
    parts = [np.where(inside, np.cos(radians), 0.0), np.where(inside, -np.sin(radians), 0.0)]
    return np.concatenate(parts, 1).astype(BF16)


def window_tables(chunks):
    count = NF // chunks
    width = window(count)
    assert width <= LANES
    out = np.zeros((chunks, width + count, LANES), np.float32)
    for chunk in range(chunks):
        start = min(max(chunk * count - SMOOTH // 2, 0), NF - width)
        bins = np.arange(start, start + width)
        radians = phases(bins, np.arange(SUB))
        out[chunk, :width, : 2 * SUB] = np.concatenate([np.cos(radians), -np.sin(radians)], 1)
        own = np.arange(chunk * count, (chunk + 1) * count)
        low = np.clip(own - SMOOTH // 2, 0, NF - SMOOTH)
        out[chunk, width:, :width] = (bins[None, :] >= low[:, None]) & (bins[None, :] < low[:, None] + SMOOTH)
    return out.astype(BF16)


def low_lanes(shape):
    return lax.broadcasted_iota(jnp.int32, shape, len(shape) - 1) % LANES < SB


def swap(value):
    return pltpu.roll(value, SB, 1)


def spread(tile):
    low = low_lanes(tile.shape)
    zero = jnp.zeros(tile.shape, F32)
    other = swap(tile)
    return [
        jnp.where(low, tile, zero),
        jnp.where(low, zero, other),
        jnp.where(low, other, zero),
        jnp.where(low, zero, tile),
    ]


def window_start(chunk, count):
    return jnp.clip(chunk * count - SMOOTH // 2, 0, NF - window(count))


def segment_kernel(sizes, x_hbm, taps_hbm, valid_hbm, table_hbm, windows_hbm, *refs):
    n_win, n_bin = sizes
    segs = n_win * n_bin
    outs, (windows_ref, x_ref, taps_ref, valid_ref, table_ref, s_ref, sem) = refs[:segs], refs[segs:]
    rows = x_hbm.shape[0]
    my_win, my_bin = lax.axis_index("win"), lax.axis_index("bin")
    x_ref[0:BACK, :] = jnp.zeros((BACK, x_ref.shape[1]), BF16)
    x_ref[BACK + rows :, :] = jnp.zeros((x_ref.shape[0] - BACK - rows, x_ref.shape[1]), BF16)
    copies = [
        pltpu.make_async_copy(x_hbm, x_ref.at[pl.ds(BACK, rows)], sem.at[0]),
        pltpu.make_async_copy(taps_hbm, taps_ref, sem.at[1]),
        pltpu.make_async_copy(valid_hbm, valid_ref, sem.at[2]),
        pltpu.make_async_copy(table_hbm, table_ref, sem.at[3]),
        pltpu.make_async_copy(windows_hbm.at[my_win * n_bin + my_bin], windows_ref, sem.at[4]),
    ]
    for copy in copies:
        copy.start()
    copies[1].wait()
    copies[0].wait()
    matrix = taps_ref[...]
    low = low_lanes((CHUNK, LANES))
    chunks = []
    for c in range(HALF // CHUNK):
        sides = []
        for start in (c * CHUNK, c * CHUNK + HALF):
            window_rows = x_ref[start : start + BACK + CHUNK, :]
            sides.append(
                jnp.concatenate([window_rows[:, t * LANES : (t + 1) * LANES] for t in range(DECIM // 2)], 0)
            )
        product = jnp.dot(matrix, jnp.concatenate(sides, 1), preferred_element_type=F32)
        product = product[0 : 2 * CHUNK] + product[2 * CHUNK :]
        even, odd = product[:CHUNK], product[CHUNK:]
        stay = jnp.where(low, even[:, :LANES], odd[:, LANES:])
        cross = jnp.where(low, even[:, LANES:], odd[:, :LANES])
        chunks.append(stay + swap(cross))
    value = jnp.concatenate(chunks, 0)
    low = low_lanes((HALF, LANES))
    zero = jnp.zeros((HALF, LANES), F32)
    other = swap(value)
    operand = jnp.concatenate(
        [
            jnp.where(low, value, zero).astype(BF16),
            jnp.where(low, other, zero).astype(BF16),
            jnp.where(low, zero, other).astype(BF16),
            jnp.where(low, zero, value).astype(BF16),
        ],
        0,
    )
    copies[3].wait()
    s_ref[...] = jnp.dot(table_ref[...], operand, preferred_element_type=F32)
    tail = swap(value[LSEG - HALF : LSEG - HALF + SUB])
    copies[2].wait()
    valid = valid_ref[...].astype(F32)
    valid = jnp.broadcast_to(jnp.concatenate([valid, valid], 1), (SUB, LANES))
    extra = jnp.where(low_lanes((SUB, LANES)), tail, valid).astype(BF16)
    count = NF // segs
    width = window(count)
    for d in range(n_win):
        for e in range(n_bin):
            chunk = lax.rem(my_win + d, n_win) * n_bin + lax.rem(my_bin + e, n_bin)
            start = pl.multiple_of(window_start(chunk, count), SUB)
            out_ref = outs[d * n_bin + e]
            out_ref[0:width, :] = s_ref[pl.ds(start, width), :].astype(BF16)
            out_ref[width:, :] = extra
    copies[4].wait()


def whiten_kernel(sizes, *refs):
    n_win, n_bin = sizes
    segs = n_win * n_bin
    parts, (windows_ref, out_ref, s_ref) = refs[:segs], refs[segs:]
    my_win, my_bin = lax.axis_index("win"), lax.axis_index("bin")
    count = NF // segs
    width = window(count)
    chunk = my_win * n_bin + my_bin
    extras = [part[width:, :].astype(F32) for part in parts]
    tails = []
    for d in range(n_win):
        for e in range(n_bin):
            win = lax.rem(my_win - d + n_win, n_win)
            core = lax.rem(my_bin - e + n_bin, n_bin)
            after = (e + 1) % n_bin
            first = core == 0
            use_same = jnp.where(first, 0.0, 1.0).astype(F32)
            use_other = jnp.where(jnp.logical_and(first, win != 0), 1.0, 0.0).astype(F32)
            same = extras[d * n_bin + after]
            other = extras[(d + 1) % n_win * n_bin + after]
            tails.append(jnp.concatenate(spread(same * use_same + other * use_other)[:2], 0).astype(BF16))
    spectra = jnp.dot(windows_ref[0:width, 0 : 2 * SUB], jnp.concatenate(tails, 1), preferred_element_type=F32)
    spectra = spectra + jnp.concatenate([part[0:width, :].astype(F32) for part in parts], 1)
    s_ref[...] = spectra
    square = spectra * spectra
    square_high = square.astype(BF16)
    square_low = (square - square_high.astype(F32)).astype(BF16)
    smooth = windows_ref[width:, 0:width]
    energy = jnp.dot(smooth, square_high, preferred_element_type=F32) + jnp.dot(
        smooth, square_low, preferred_element_type=F32
    )
    own = pl.multiple_of(chunk * count - window_start(chunk, count), SUB)
    whites = []
    for s in range(segs):
        at = slice(s * LANES, (s + 1) * LANES)
        total = energy[:, at] + swap(energy[:, at])
        valid = extras[s][0:1]
        valid = jnp.where(low_lanes((1, LANES)), swap(valid), valid)
        scale = valid * lax.rsqrt(total * (1.0 / (2.0 * SMOOTH)) + EPSILON)
        whites.append(s_ref[pl.ds(own, count), at] * scale)
    for g in range(count // SUB):
        tiles = [white[SUB * g : SUB * g + SUB] for white in whites]
        out_ref[SUB * segs * g : SUB * segs * (g + 1), :] = jnp.concatenate(tiles, 0).astype(BF16)


def operands(values):
    left, right = [], []
    for s in range(values.shape[0] // SUB):
        real_even, real_odd, imag_even, imag_odd = spread(values[SUB * s : SUB * s + SUB])
        left += [real_even, real_odd, imag_even, imag_odd]
        right += [-imag_even, -imag_odd, real_even, real_odd]
    return jnp.concatenate(left, 0), jnp.concatenate(right, 0)


def home_kernel(factor, home_ref, out_ref):
    groups, rows, depth = out_ref.shape
    row = lax.broadcasted_iota(jnp.int32, (rows, LANES), 0)
    lane = lax.broadcasted_iota(jnp.int32, (rows, LANES), 1)
    pick = jnp.where(lane % SB == 2 * (row // SUB) + lane // SB, factor, 0.0).astype(BF16)
    row = lax.broadcasted_iota(jnp.int32, (rows, depth), 0)
    lane = lax.broadcasted_iota(jnp.int32, (rows, depth), 1)
    diagonal = row % SUB == lane % SUB
    size = home_ref.shape[0] // groups
    for g in range(groups):
        left, _ = operands(home_ref[size * g : size * (g + 1), :].astype(F32))
        turned = lax.dot_general(pick, left.astype(BF16), (((1,), (1,)), ((), ())), preferred_element_type=F32)
        out_ref[g] = jnp.where(diagonal, turned, 0.0).astype(BF16)


def cross_kernel(offset, factor, home_ref, away_ref, *refs):
    out_hbm, out_ref, sem = refs[-3:]
    groups = home_ref.shape[0]
    size = away_ref.shape[0] // groups
    unroll = 5 if groups % 5 == 0 else 1

    def copy(g, c):
        at = pl.ds(pl.multiple_of(SUB * g, SUB), SUB)
        return pltpu.make_async_copy(out_ref.at[c, at], out_hbm.at[offset, 0, c, at], sem.at[2 * g + c])

    def some(k, _):
        for g in [k * unroll + j for j in range(unroll)]:
            values = away_ref[pl.ds(pl.multiple_of(size * g, size), size), :].astype(F32)
            block = jnp.concatenate(operands(values), 1).astype(BF16)
            product = jnp.dot(home_ref[g], block, preferred_element_type=F32)
            if factor != 1.0:
                product = product * factor
            at = pl.ds(pl.multiple_of(SUB * g, SUB), SUB)
            for c in range(2):
                for t in range(SB // 2):
                    out_ref[c, at, t * LANES : (t + 1) * LANES] = product[
                        SUB * t : SUB * t + SUB, c * LANES : (c + 1) * LANES
                    ]
                copy(g, c).start()
        return 0

    lax.fori_loop(0, groups // unroll, some, 0)
    for g in range(groups):
        for c in range(2):
            copy(g, c).wait()


def shifted(value, axis, steps):
    size = lax.axis_size(axis)
    return lax.ppermute(value, axis, [(i, (i + steps) % size) for i in range(size)])


def cost(flops, moved):
    return pl.CostEstimate(flops=int(flops), bytes_accessed=int(moved), transcendentals=0)


def room(limit):
    return pltpu.CompilerParams(vmem_limit_bytes=limit)


VMEM = pl.BlockSpec(memory_space=pltpu.VMEM)
HBM = pl.BlockSpec(memory_space=pl.ANY)


def per_device(raw_counts, seg_valid):
    n_win, n_bin = lax.axis_size("win"), lax.axis_size("bin")
    segs = n_win * n_bin
    samples = raw_counts[:, 0, :]
    rows = samples.shape[0]
    assert rows == LSEG and NF % (SUB * segs) == 0
    bins = NF // segs
    groups = bins // SUB
    rows_sent = window(bins) + SUB
    matrix, table, windows = (jnp.asarray(t) for t in (tap_matrix(), transform_table(), window_tables(segs)))
    *sent, own_window = pl.pallas_call(
        functools.partial(segment_kernel, (n_win, n_bin)),
        out_shape=(jax.ShapeDtypeStruct((rows_sent, LANES), BF16),) * segs
        + (jax.ShapeDtypeStruct(windows.shape[1:], BF16),),
        in_specs=[pl.BlockSpec(memory_space=pltpu.HBM)] * 5,
        out_specs=(VMEM,) * (segs + 1),
        scratch_shapes=[
            pltpu.VMEM((BACK + 2 * HALF, samples.shape[1]), BF16),
            pltpu.VMEM(matrix.shape, BF16),
            pltpu.VMEM(seg_valid.shape, jnp.int32),
            pltpu.VMEM(table.shape, BF16),
            pltpu.VMEM((NF, LANES), F32),
            pltpu.SemaphoreType.DMA((5,)),
        ],
        cost_estimate=cost(8 * samples.size * 2 * LANES, 2 * (samples.size + table.size)),
        compiler_params=room(16 << 20),
        name="segment",
    )(*(pltpu.with_memory_space_constraint(v, pltpu.HBM) for v in (samples, matrix, seg_valid, table, windows)))

    parts = [sent[0]] + [None] * (segs - 1)
    for d in reversed(range(n_win)):
        for e in range(n_bin):
            if d or e:
                route = [
                    (w * n_bin + c, (w + d) % n_win * n_bin + (c + e) % n_bin) for w in range(n_win) for c in range(n_bin)
                ]
                parts[d * n_bin + e] = lax.ppermute(sent[d * n_bin + e], ("win", "bin"), route)
    home = pl.pallas_call(
        functools.partial(whiten_kernel, (n_win, n_bin)),
        out_shape=jax.ShapeDtypeStruct((segs * bins, LANES), BF16),
        in_specs=[VMEM] * (segs + 1),
        out_specs=VMEM,
        scratch_shapes=[pltpu.VMEM((window(bins), segs * LANES), F32)],
        cost_estimate=cost(4 * bins * window(bins) * segs * LANES, 8 * segs * bins * LANES),
        compiler_params=room(6 << 20),
        name="whiten",
    )(*parts, own_window)

    aways = [shifted(home, "blk", offset) for offset in range(1, ROUNDS + 1)]
    depth = segs * 4 * SUB
    tall = SB // 2 * SUB
    early = 1.0 / segs if segs & (segs - 1) == 0 else 1.0
    turned = pl.pallas_call(
        functools.partial(home_kernel, early),
        out_shape=jax.ShapeDtypeStruct((groups, tall, depth), BF16),
        in_specs=[VMEM],
        out_specs=VMEM,
        cost_estimate=cost(2 * groups * tall * depth * LANES, 2 * groups * tall * depth),
        compiler_params=room(6 << 20),
        name="home",
    )(home)

    stacks = None
    for offset in range(ROUNDS):
        extra = [] if stacks is None else [stacks]
        stacks = pl.pallas_call(
            functools.partial(cross_kernel, offset, 1.0 / segs / early),
            out_shape=jax.ShapeDtypeStruct((ROUNDS, 1, 2, bins, SB * SB), F32),
            in_specs=[VMEM] * 2 + [HBM] * len(extra),
            out_specs=HBM,
            scratch_shapes=[pltpu.VMEM((2, bins, SB * SB), F32), pltpu.SemaphoreType.DMA((2 * groups,))],
            input_output_aliases={2: 0} if extra else {},
            cost_estimate=cost(4 * groups * tall * depth * LANES, 8 * bins * SB * SB),
            compiler_params=room(8 << 20),
            name="cross",
        )(turned, aways[offset], *extra)
    return stacks


def solution(mesh):
    in_specs = (P(("win", "bin"), ("parts", "blk"), None), P(("win", "bin"), ("parts", "blk")))
    out_specs = P(None, ("parts", "blk"), None, ("win", "bin"), None)
    return jax.shard_map(per_device, mesh=mesh, in_specs=in_specs, out_specs=out_specs, check_vma=False)
```

```python
import functools
import math

import jax
import jax.numpy as jnp
import numpy as np
from jax import lax
from jax.experimental import pallas as pl
from jax.experimental.pallas import tpu as pltpu
from jax.sharding import PartitionSpec as P

SB = 64
LSEG = 600
NF = 320
DECIM = 10
TAPS = 64
SMOOTH = 33
ROUNDS = 2
HIST = 7

EPSILON = 1e-06
LANES = 128
SUB = 8
HALF = 320
CHUNK = 32
BACK = 16
BF16 = jnp.bfloat16
F32 = jnp.float32


def filter_coeffs():
    position = np.arange(TAPS, dtype=np.float64)
    centre = 0.5 * (TAPS - 1)
    cutoff = 0.4 / DECIM
    shaped = np.sinc(2.0 * cutoff * (position - centre))
    window = 0.54 - 0.46 * np.cos(2.0 * math.pi * position / (TAPS - 1))
    return 2.0 * cutoff * shaped * window


def taps():
    coeffs = filter_coeffs()
    weights = np.zeros((DECIM, HIST + 1), np.float32)
    for p in range(DECIM):
        for o in range(HIST + 1):
            t = DECIM * o - p
            if 0 <= t < TAPS:
                weights[p, o] = coeffs[t]
    high = weights.astype(BF16).astype(np.float32)
    low = (weights - high).astype(BF16).astype(np.float32)
    return high, low


def tap_matrix():
    out = np.zeros((2, 2, CHUNK, DECIM // 2, BACK + CHUNK), np.float32)
    for part, values in enumerate(taps()):
        for p in range(DECIM):
            for o in range(HIST + 1):
                for n in range(CHUNK):
                    out[part, p % 2, n, p // 2, BACK + n - o] = values[p, o]
    return out.reshape(4 * CHUNK, DECIM // 2 * (BACK + CHUNK)).astype(BF16)


def window(count):
    return count + SMOOTH - 1


def phases(bins, samples):
    return ((bins[:, None] + 1) * samples[None, :] % (2 * LSEG)) * (math.pi / LSEG)


def transform_table():
    samples = np.arange(2 * HALF)
    radians = phases(np.arange(NF), samples)
    inside = samples[None, :] < LSEG
    parts = [np.where(inside, np.cos(radians), 0.0), np.where(inside, -np.sin(radians), 0.0)]
    return np.concatenate(parts, 1).astype(BF16)


def window_tables(chunks):
    count = NF // chunks
    width = window(count)
    assert width <= LANES
    out = np.zeros((chunks, width + count, 2 * LANES), np.float32)
    for chunk in range(chunks):
        start = min(max(chunk * count - SMOOTH // 2, 0), NF - width)
        bins = np.arange(start, start + width)
        radians = phases(bins, np.arange(SUB))
        out[chunk, :width, : 2 * SUB] = np.concatenate([np.cos(radians), -np.sin(radians)], 1)
        own = np.arange(chunk * count, (chunk + 1) * count)
        low = np.clip(own - SMOOTH // 2, 0, NF - SMOOTH)
        inside = (bins[None, :] >= low[:, None]) & (bins[None, :] < low[:, None] + SMOOTH)
        out[chunk, width:, : 2 * width] = np.concatenate([inside, inside], 1)
    return out.astype(BF16)


def low_lanes(shape):
    return lax.broadcasted_iota(jnp.int32, shape, len(shape) - 1) % LANES < SB


def swap(value):
    return pltpu.roll(value, SB, 1)


def spread(tile):
    low = low_lanes(tile.shape)
    zero = jnp.zeros(tile.shape, F32)
    other = swap(tile)
    return [
        jnp.where(low, tile, zero),
        jnp.where(low, zero, other),
        jnp.where(low, other, zero),
        jnp.where(low, zero, tile),
    ]


def window_start(chunk, count):
    return jnp.clip(chunk * count - SMOOTH // 2, 0, NF - window(count))


def segment_kernel(sizes, x_hbm, taps_hbm, valid_hbm, table_hbm, windows_hbm, *refs):
    n_win, n_bin = sizes
    segs = n_win * n_bin
    outs, (windows_ref, x_ref, taps_ref, valid_ref, table_ref, s_ref, sem) = refs[:segs], refs[segs:]
    rows = x_hbm.shape[0]
    my_win, my_bin = lax.axis_index("win"), lax.axis_index("bin")
    copies = [
        pltpu.make_async_copy(x_hbm, x_ref.at[pl.ds(BACK, rows)], sem.at[0]),
        pltpu.make_async_copy(taps_hbm, taps_ref, sem.at[1]),
        pltpu.make_async_copy(valid_hbm, valid_ref, sem.at[2]),
        pltpu.make_async_copy(table_hbm, table_ref, sem.at[3]),
        pltpu.make_async_copy(windows_hbm.at[my_win * n_bin + my_bin], windows_ref, sem.at[4]),
    ]
    for copy in copies:
        copy.start()
    x_ref[0:BACK, :] = jnp.zeros((BACK, x_ref.shape[1]), BF16)
    x_ref[BACK + rows :, :] = jnp.zeros((x_ref.shape[0] - BACK - rows, x_ref.shape[1]), BF16)
    copies[1].wait()
    copies[0].wait()
    matrix = taps_ref[...]
    low = low_lanes((CHUNK, LANES))
    chunks = []
    for c in range(HALF // CHUNK):
        sides = []
        for start in (c * CHUNK, c * CHUNK + HALF):
            window_rows = x_ref[start : start + BACK + CHUNK, :]
            sides.append(
                jnp.concatenate([window_rows[:, t * LANES : (t + 1) * LANES] for t in range(DECIM // 2)], 0)
            )
        product = jnp.dot(matrix, jnp.concatenate(sides, 1), preferred_element_type=F32)
        product = product[0 : 2 * CHUNK] + product[2 * CHUNK :]
        even, odd = product[:CHUNK], product[CHUNK:]
        stay = jnp.where(low, even[:, :LANES], odd[:, LANES:])
        cross = jnp.where(low, even[:, LANES:], odd[:, :LANES])
        chunks.append(stay + swap(cross))
    value = jnp.concatenate(chunks, 0)
    low = low_lanes((HALF, LANES))
    zero = jnp.zeros((HALF, LANES), F32)
    other = swap(value)
    operand = jnp.concatenate(
        [
            jnp.where(low, value, zero).astype(BF16),
            jnp.where(low, other, zero).astype(BF16),
            jnp.where(low, zero, other).astype(BF16),
            jnp.where(low, zero, value).astype(BF16),
        ],
        0,
    )
    copies[3].wait()
    s_ref[...] = jnp.dot(table_ref[...], operand, preferred_element_type=F32)
    tail = swap(value[LSEG - HALF : LSEG - HALF + SUB])
    copies[2].wait()
    valid = valid_ref[...].astype(F32)
    valid = jnp.broadcast_to(jnp.concatenate([valid, valid], 1), (SUB, LANES))
    extra = jnp.where(low_lanes((SUB, LANES)), tail, valid).astype(BF16)
    count = NF // segs
    width = window(count)
    for d in range(n_win):
        for e in range(n_bin):
            chunk = lax.rem(my_win + d, n_win) * n_bin + lax.rem(my_bin + e, n_bin)
            start = pl.multiple_of(window_start(chunk, count), SUB)
            out_ref = outs[d * n_bin + e]
            out_ref[0:width, :] = s_ref[pl.ds(start, width), :].astype(BF16)
            out_ref[width:, :] = extra
    copies[4].wait()


def whiten_kernel(sizes, *refs):
    n_win, n_bin = sizes
    segs = n_win * n_bin
    parts, (windows_ref, out_ref, s_ref) = refs[:segs], refs[segs:]
    my_win, my_bin = lax.axis_index("win"), lax.axis_index("bin")
    count = NF // segs
    width = window(count)
    chunk = my_win * n_bin + my_bin
    extras = [part[width:, :].astype(F32) for part in parts]
    tails = []
    for d in range(n_win):
        for e in range(n_bin):
            win = lax.rem(my_win - d + n_win, n_win)
            core = lax.rem(my_bin - e + n_bin, n_bin)
            after = (e + 1) % n_bin
            first = core == 0
            use_same = jnp.where(first, 0.0, 1.0).astype(F32)
            use_other = jnp.where(jnp.logical_and(first, win != 0), 1.0, 0.0).astype(F32)
            same = extras[d * n_bin + after]
            other = extras[(d + 1) % n_win * n_bin + after]
            tails.append(jnp.concatenate(spread(same * use_same + other * use_other)[:2], 0).astype(BF16))
    spectra = jnp.dot(windows_ref[0:width, 0 : 2 * SUB], jnp.concatenate(tails, 1), preferred_element_type=F32)
    spectra = spectra + jnp.concatenate([part[0:width, :].astype(F32) for part in parts], 1)
    s_ref[...] = spectra
    square = spectra * spectra
    square_high = square.astype(BF16)
    square_low = (square - square_high.astype(F32)).astype(BF16)
    parts_of_square = jnp.concatenate([square_high, square_low], 0)
    energy = jnp.dot(windows_ref[width:, 0 : 2 * width], parts_of_square, preferred_element_type=F32)
    own = pl.multiple_of(chunk * count - window_start(chunk, count), SUB)
    whites = []
    for s in range(segs):
        at = slice(s * LANES, (s + 1) * LANES)
        total = energy[:, at] + swap(energy[:, at])
        valid = extras[s][0:1]
        valid = jnp.where(low_lanes((1, LANES)), swap(valid), valid)
        scale = valid * lax.rsqrt(total * (1.0 / (2.0 * SMOOTH)) + EPSILON)
        whites.append(s_ref[pl.ds(own, count), at] * scale)
    for g in range(count // SUB):
        tiles = [white[SUB * g : SUB * g + SUB] for white in whites]
        out_ref[SUB * segs * g : SUB * segs * (g + 1), :] = jnp.concatenate(tiles, 0).astype(BF16)


def operands(values):
    left, right = [], []
    for s in range(values.shape[0] // SUB):
        real_even, real_odd, imag_even, imag_odd = spread(values[SUB * s : SUB * s + SUB])
        left += [real_even, real_odd, imag_even, imag_odd]
        right += [-imag_even, -imag_odd, real_even, real_odd]
    return jnp.concatenate(left, 0), jnp.concatenate(right, 0)


def home_kernel(factor, home_ref, out_ref):
    groups, rows, depth = out_ref.shape
    row = lax.broadcasted_iota(jnp.int32, (rows, LANES), 0)
    lane = lax.broadcasted_iota(jnp.int32, (rows, LANES), 1)
    pick = jnp.where(lane % SB == 2 * (row // SUB) + lane // SB, factor, 0.0).astype(BF16)
    row = lax.broadcasted_iota(jnp.int32, (rows, depth), 0)
    lane = lax.broadcasted_iota(jnp.int32, (rows, depth), 1)
    diagonal = row % SUB == lane % SUB
    size = home_ref.shape[0] // groups
    for g in range(groups):
        left, _ = operands(home_ref[size * g : size * (g + 1), :].astype(F32))
        turned = lax.dot_general(pick, left.astype(BF16), (((1,), (1,)), ((), ())), preferred_element_type=F32)
        out_ref[g] = jnp.where(diagonal, turned, 0.0).astype(BF16)


def cross_kernel(offset, factor, home_ref, away_ref, *refs):
    out_hbm, out_ref, sem = refs[-3:]
    groups = home_ref.shape[0]
    size = away_ref.shape[0] // groups
    unroll = 5 if groups % 5 == 0 else 1

    def copy(g, c):
        at = pl.ds(pl.multiple_of(SUB * g, SUB), SUB)
        return pltpu.make_async_copy(out_ref.at[c, at], out_hbm.at[offset, 0, c, at], sem.at[2 * g + c])

    def some(k, _):
        for g in [k * unroll + j for j in range(unroll)]:
            values = away_ref[pl.ds(pl.multiple_of(size * g, size), size), :].astype(F32)
            block = jnp.concatenate(operands(values), 1).astype(BF16)
            product = jnp.dot(home_ref[g], block, preferred_element_type=F32)
            if factor != 1.0:
                product = product * factor
            at = pl.ds(pl.multiple_of(SUB * g, SUB), SUB)
            for c in range(2):
                for t in range(SB // 2):
                    out_ref[c, at, t * LANES : (t + 1) * LANES] = product[
                        SUB * t : SUB * t + SUB, c * LANES : (c + 1) * LANES
                    ]
                copy(g, c).start()
        return 0

    lax.fori_loop(0, groups // unroll, some, 0)
    for g in range(groups):
        for c in range(2):
            copy(g, c).wait()


def shifted(value, axis, steps):
    size = lax.axis_size(axis)
    return lax.ppermute(value, axis, [(i, (i + steps) % size) for i in range(size)])


def cost(flops, moved):
    return pl.CostEstimate(flops=int(flops), bytes_accessed=int(moved), transcendentals=0)


def room(limit):
    return pltpu.CompilerParams(vmem_limit_bytes=limit)


VMEM = pl.BlockSpec(memory_space=pltpu.VMEM)
HBM = pl.BlockSpec(memory_space=pl.ANY)


def per_device(raw_counts, seg_valid):
    n_win, n_bin = lax.axis_size("win"), lax.axis_size("bin")
    segs = n_win * n_bin
    samples = raw_counts[:, 0, :]
    rows = samples.shape[0]
    assert rows == LSEG and NF % (SUB * segs) == 0
    bins = NF // segs
    groups = bins // SUB
    rows_sent = window(bins) + SUB
    matrix, table, windows = (jnp.asarray(t) for t in (tap_matrix(), transform_table(), window_tables(segs)))
    *sent, own_window = pl.pallas_call(
        functools.partial(segment_kernel, (n_win, n_bin)),
        out_shape=(jax.ShapeDtypeStruct((rows_sent, LANES), BF16),) * segs
        + (jax.ShapeDtypeStruct(windows.shape[1:], BF16),),
        in_specs=[pl.BlockSpec(memory_space=pltpu.HBM)] * 5,
        out_specs=(VMEM,) * (segs + 1),
        scratch_shapes=[
            pltpu.VMEM((BACK + 2 * HALF, samples.shape[1]), BF16),
            pltpu.VMEM(matrix.shape, BF16),
            pltpu.VMEM(seg_valid.shape, jnp.int32),
            pltpu.VMEM(table.shape, BF16),
            pltpu.VMEM((NF, LANES), F32),
            pltpu.SemaphoreType.DMA((5,)),
        ],
        cost_estimate=cost(8 * samples.size * 2 * LANES, 2 * (samples.size + table.size)),
        compiler_params=room(16 << 20),
        name="segment",
    )(*(pltpu.with_memory_space_constraint(v, pltpu.HBM) for v in (samples, matrix, seg_valid, table, windows)))

    parts = [sent[0]] + [None] * (segs - 1)
    for d in reversed(range(n_win)):
        for e in range(n_bin):
            if d or e:
                route = [
                    (w * n_bin + c, (w + d) % n_win * n_bin + (c + e) % n_bin) for w in range(n_win) for c in range(n_bin)
                ]
                parts[d * n_bin + e] = lax.ppermute(sent[d * n_bin + e], ("win", "bin"), route)
    home = pl.pallas_call(
        functools.partial(whiten_kernel, (n_win, n_bin)),
        out_shape=jax.ShapeDtypeStruct((segs * bins, LANES), BF16),
        in_specs=[VMEM] * (segs + 1),
        out_specs=VMEM,
        scratch_shapes=[pltpu.VMEM((window(bins), segs * LANES), F32)],
        cost_estimate=cost(4 * bins * window(bins) * segs * LANES, 8 * segs * bins * LANES),
        compiler_params=room(6 << 20),
        name="whiten",
    )(*parts, own_window)

    aways = [shifted(home, "blk", offset) for offset in range(1, ROUNDS + 1)]
    depth = segs * 4 * SUB
    tall = SB // 2 * SUB
    early = 1.0 / segs if segs & (segs - 1) == 0 else 1.0
    turned = pl.pallas_call(
        functools.partial(home_kernel, early),
        out_shape=jax.ShapeDtypeStruct((groups, tall, depth), BF16),
        in_specs=[VMEM],
        out_specs=VMEM,
        cost_estimate=cost(2 * groups * tall * depth * LANES, 2 * groups * tall * depth),
        compiler_params=room(6 << 20),
        name="home",
    )(home)

    stacks = None
    for offset in range(ROUNDS):
        extra = [] if stacks is None else [stacks]
        stacks = pl.pallas_call(
            functools.partial(cross_kernel, offset, 1.0 / segs / early),
            out_shape=jax.ShapeDtypeStruct((ROUNDS, 1, 2, bins, SB * SB), F32),
            in_specs=[VMEM] * 2 + [HBM] * len(extra),
            out_specs=HBM,
            scratch_shapes=[pltpu.VMEM((2, bins, SB * SB), F32), pltpu.SemaphoreType.DMA((2 * groups,))],
            input_output_aliases={2: 0} if extra else {},
            cost_estimate=cost(4 * groups * tall * depth * LANES, 8 * bins * SB * SB),
            compiler_params=room(8 << 20),
            name="cross",
        )(turned, aways[offset], *extra)
    return stacks


def solution(mesh):
    in_specs = (P(("win", "bin"), ("parts", "blk"), None), P(("win", "bin"), ("parts", "blk")))
    out_specs = P(None, ("parts", "blk"), None, ("win", "bin"), None)
    return jax.shard_map(per_device, mesh=mesh, in_specs=in_specs, out_specs=out_specs, check_vma=False)
```
